512 devices in a mesh: group: 128 (over z, y, core), mp: 4 (over x).
Axes of the slice: x: 4, y: 8, z: 8, core: 2. Of those that a mesh axis runs over, the one named last changes fastest.
Arguments:
- observations: bfloat16 [16384, 512], P('group', 'mp'), may hold values from -6 to 6
- hidden_state: bfloat16 [8192, 1024], P('group', 'mp'), may hold values from -0.8984375 to 0.8984375
- cell_state: bfloat16 [8192, 1024], P('group', 'mp'), may hold values from -4 to 4
- arrival_order: int32 [8192], replicated, may hold values from 0 to 8191, as said below
- batch_counts: int32 [128], replicated, may hold values from 0 to 128, as said below
- input_weight: bfloat16 [512, 4, 1024], P(None, None, 'mp'), may hold values from -0.15625 to 0.15625
- state_weight: bfloat16 [1024, 4, 1024], P(None, None, 'mp'), may hold values from -0.15625 to 0.15625
- gate_bias: float32 [4, 1024], P(None, 'mp'), may hold values from -3 to 3
- head_weight: bfloat16 [1024, 2, 512], P(None, None, 'mp'), may hold values from -0.1875 to 0.1875
- head_bias: float32 [2, 512], P(None, 'mp'), may hold values from -3 to 3
- value_weight: bfloat16 [512, 1], P('mp'), may hold values from -0.25 to 0.25
- value_bias: float32 [1], replicated, may hold values from -3 to 3
- advantage_weight: bfloat16 [512, 18], P('mp'), may hold values from -0.25 to 0.25
- advantage_bias: float32 [18], replicated, may hold values from -3 to 3
Outputs:
- action_values: float32 [16384, 18], P('group')
- new_hidden: bfloat16 [8192, 1024], P('group', 'mp')
- new_cell: bfloat16 [8192, 1024], P('group', 'mp')
The draws below stay inside these ranges and needn't reach their ends.
Inputs may be any that keep to these rules, and one draw needn't show every extreme that they name: `arrival_order`: A permutation: each actor id once. Positions starts[b] to starts[b] + batch_counts[b] - 1 hold the actors of batch b, where starts is the running sum of batch_counts. Of the actors of one owner (ids k * 64 to (k + 1) * 64 - 1), at most 1 lie in one batch. `batch_counts`: sums to 8192.
All inputs are finite; a program needn't handle non-finite values.
Results may differ from the reference program's by a relative error of at most 0.0019.
Values may be sent and summed in bfloat16 or wider, within the bound.
A program may use at most 64 MiB of HBM per device.

```python
import jax
import jax.numpy as jnp

H = 1024
FEAT = 512
HEADH = 512
NACT = 18
ACT_DEV = 64
ACTORS = 8192
BATCHES = 128
CAPB = 128
PEER = 1


def layout(key):
    base_key = jax.random.fold_in(key, 7)
    busiest = jax.random.randint(jax.random.fold_in(base_key, 1), (), 0, BATCHES)
    slot_total = BATCHES * PEER
    slot_batch = jnp.arange(slot_total, dtype=jnp.int32) // PEER

    def owner_pick(owner_key):
        slot_ranks = jax.random.permutation(jax.random.fold_in(owner_key, 2), slot_total).astype(jnp.int32)
        slot_ranks = jnp.where(slot_batch == busiest, slot_ranks - slot_total, slot_ranks)
        chosen = jnp.argsort(slot_ranks, stable=True)[:ACT_DEV]
        shuffle = jax.random.permutation(jax.random.fold_in(owner_key, 3), ACT_DEV)
        return slot_batch[chosen][shuffle]
    owner_keys = jax.random.split(jax.random.fold_in(base_key, 4), BATCHES)
    batch_of = jax.vmap(owner_pick)(owner_keys).reshape(ACTORS).astype(jnp.int32)
    tie_break = jax.random.permutation(jax.random.fold_in(base_key, 5), ACTORS).astype(jnp.int32)
    arrival = jnp.argsort(batch_of * ACTORS + tie_break, stable=True).astype(jnp.int32)
    tallies = jnp.sum((batch_of[None, :] == jnp.arange(BATCHES, dtype=jnp.int32)[:, None]).astype(jnp.int32), axis=1).astype(jnp.int32)
    return (arrival, tallies)


def draw_arrival_order(key, part):
    return layout(key)[0]


def draw_batch_counts(key, part):
    return layout(key)[1]


def shard_levels(own_key, shape, cuts, least, top_value):
    def one(dim, parts):
        draws = jax.random.uniform(jax.random.fold_in(jax.random.fold_in(own_key, 6), dim), (parts,), jnp.float32, least / len(cuts), top_value / len(cuts))
        return jnp.repeat(jnp.exp(draws), shape[dim] // parts).reshape((-1,) + (1,) * (len(shape) - dim - 1))

    factor_of = one(*cuts[0])
    for cut in cuts[1:]:
        factor_of = factor_of * one(*cut)
    return factor_of


def gaussian(rng, shape, width, bound, cuts=(), held_as=jnp.bfloat16):
    gain = shard_levels(rng, shape, cuts, -0.22, 0.18) if cuts else 1.0
    entries = jax.random.normal(rng, shape, jnp.float32) * width * gain
    return jnp.minimum(jnp.maximum(entries, -bound), bound).astype(held_as)


def setup_inputs(seed: int = 0) -> dict:
    arg_keys = jax.random.split(jax.random.key(seed), 15)
    observations = gaussian(arg_keys[0], (BATCHES * CAPB, FEAT), 1.0, 6.0, ((0, 128), (1, 4)))
    hidden_state = jnp.clip(jax.random.uniform(arg_keys[1], (ACTORS, H), jnp.float32, -0.8984375, 0.8984375) * shard_levels(arg_keys[1], (ACTORS, H), ((0, 128), (1, 4)), -0.4, 0.0), -0.8984375, 0.8984375).astype(jnp.bfloat16)
    cell_state = gaussian(arg_keys[2], (ACTORS, H), 1.0, 4.0, ((0, 128), (1, 4)))
    arrival_order = draw_arrival_order(jax.random.fold_in(arg_keys[14], 71), 0)
    batch_counts = draw_batch_counts(jax.random.fold_in(arg_keys[14], 71), 0)
    input_weight = gaussian(arg_keys[5], (FEAT, 4, H), (FEAT + H) ** -0.5, 0.15625, ((2, 4),))
    state_weight = gaussian(arg_keys[6], (H, 4, H), (FEAT + H) ** -0.5, 0.15625, ((2, 4),))
    gate_bias = gaussian(arg_keys[7], (4, H), 0.5, 3.0, ((1, 4),), jnp.float32)
    head_weight = gaussian(arg_keys[8], (H, 2, HEADH), H ** -0.5, 0.1875, ((2, 4),))
    head_bias = gaussian(arg_keys[9], (2, HEADH), 0.5, 3.0, ((1, 4),), jnp.float32)
    value_weight = gaussian(arg_keys[10], (HEADH, 1), HEADH ** -0.5, 0.25, ((0, 4),))
    value_bias = gaussian(arg_keys[11], (1,), 1.0, 3.0, (), jnp.float32)
    advantage_weight = gaussian(arg_keys[12], (HEADH, NACT), HEADH ** -0.5, 0.25, ((0, 4),))
    advantage_bias = gaussian(arg_keys[13], (NACT,), 1.0, 3.0, (), jnp.float32)
    return dict(observations=observations, hidden_state=hidden_state, cell_state=cell_state, arrival_order=arrival_order, batch_counts=batch_counts, input_weight=input_weight, state_weight=state_weight, gate_bias=gate_bias, head_weight=head_weight, head_bias=head_bias, value_weight=value_weight, value_bias=value_bias, advantage_weight=advantage_weight, advantage_bias=advantage_bias)


def reference(observations, hidden_state, cell_state, arrival_order, batch_counts, input_weight, state_weight, gate_bias, head_weight, head_bias, value_weight, value_bias, advantage_weight, advantage_bias):
    batch_ends = jnp.cumsum(batch_counts).astype(jnp.int32)
    batch_starts = (batch_ends - batch_counts).astype(jnp.int32)
    position = jnp.zeros((ACTORS,), jnp.int32).at[arrival_order].set(jnp.arange(ACTORS, dtype=jnp.int32))
    batch_index = jnp.sum((position[:, None] >= batch_ends[None, :]).astype(jnp.int32), axis=1).astype(jnp.int32)
    obs_row = (batch_index * CAPB + position - batch_starts[batch_index]).astype(jnp.int32)
    obs_rows = observations[obs_row]
    gate_values = jnp.dot(obs_rows, input_weight.reshape(FEAT, 4 * H), preferred_element_type=jnp.float32)
    gate_values = gate_values + jnp.dot(hidden_state, state_weight.reshape(H, 4 * H), preferred_element_type=jnp.float32)
    gate_values = gate_values.reshape(ACTORS, 4, H) + gate_bias[None]
    cell_next = jax.nn.sigmoid(gate_values[:, 1]) * cell_state.astype(jnp.float32) + jax.nn.sigmoid(gate_values[:, 0]) * jnp.tanh(gate_values[:, 2])
    hidden_next = (jax.nn.sigmoid(gate_values[:, 3]) * jnp.tanh(cell_next)).astype(jnp.bfloat16)
    stream = jnp.dot(hidden_next, head_weight.reshape(H, 2 * HEADH), preferred_element_type=jnp.float32)
    stream = jax.nn.relu(stream.reshape(ACTORS, 2, HEADH) + head_bias[None]).astype(jnp.bfloat16)
    value_sum = jnp.dot(stream[:, 0], value_weight, preferred_element_type=jnp.float32) + value_bias
    advantage_sum = jnp.dot(stream[:, 1], advantage_weight, preferred_element_type=jnp.float32) + advantage_bias
    slot_values = value_sum + advantage_sum - jnp.mean(advantage_sum, axis=1, keepdims=True)
    action_values = jnp.zeros((BATCHES * CAPB, NACT), jnp.float32).at[obs_row].set(slot_values)
    return action_values, hidden_next, cell_next.astype(jnp.bfloat16)
```

```python
import functools

import jax
import jax.numpy as jnp
from jax import lax
from jax.experimental import pallas as pl
from jax.experimental.pallas import tpu as pltpu
from jax.sharding import PartitionSpec as P

MESH = pl.DeviceIdType.MESH
F32 = jnp.float32
BF16 = jnp.bfloat16
NT = (((1,), (1,)), ((), ()))
TN = (((0,), (0,)), ((), ()))


def iota(shape, dim):
    return lax.broadcasted_iota(jnp.int32, shape, dim)


def dot(a, b, dims=(((1,), (0,)), ((), ()))):
    return lax.dot_general(a, b, dims, preferred_element_type=F32)


def pick(table, values, dims):
    high = values.astype(BF16)
    rest = values - high.astype(F32)
    mid = rest.astype(BF16)
    low = (rest - mid.astype(F32)).astype(BF16)
    return dot(table, high, dims) + dot(table, mid, dims) + dot(table, low, dims)


def step_kernel(
    groups,
    parts,
    obs_ref,
    hidden_ref,
    cell_ref,
    order_ref,
    counts_ref,
    wi_hbm,
    ws_hbm,
    gate_bias_ref,
    wh_hbm,
    head_bias_ref,
    value_weight_ref,
    value_bias_ref,
    adv_weight_ref,
    adv_bias_ref,
    q_out,
    hidden_out,
    cell_out,
    wi,
    ws,
    wh,
    obs_send,
    obs_recv,
    obs_all,
    hid_all,
    new_all,
    part_all,
    val_send,
    val_recv,
    wsem,
    gsem,
    xsem,
):
    me = lax.axis_index("group")
    x = lax.axis_index("mp")
    own = hidden_ref.shape[0]
    slots = obs_ref.shape[0]
    units = cell_ref.shape[1]
    head_units = head_bias_ref.shape[1]
    actions = adv_weight_ref.shape[1]

    barrier = pltpu.get_barrier_semaphore()

    def greet(k, carry):
        pl.semaphore_signal(
            barrier, inc=1, device_id=(lax.rem(me + k, groups), x), device_id_type=MESH
        )
        return carry

    lax.fori_loop(1, groups, greet, 0)
    for k in range(1, parts):
        pl.semaphore_signal(
            barrier, inc=1, device_id=(me, lax.rem(x + k, parts)), device_id_type=MESH
        )

    loads = [
        pltpu.make_async_copy(a, b, wsem.at[i])
        for i, (a, b) in enumerate(((ws_hbm, ws), (wi_hbm, wi), (wh_hbm, wh)))
    ]
    for load in loads:
        load.start()

    counts = jnp.broadcast_to(counts_ref[...], (8, groups))
    before = (iota((groups, groups), 0) < iota((groups, groups), 1)).astype(BF16)
    starts = dot(counts.astype(BF16), before).astype(jnp.int32)[0:1]
    ends = starts + counts[0:1]
    mine = iota((1, groups), 1) == me
    start = jnp.sum(jnp.where(mine, starts, 0), axis=1, keepdims=True)
    count = jnp.sum(jnp.where(mine, counts[0:1], 0), axis=1, keepdims=True)
    order = order_ref[...]
    rows = order.shape[0]
    first = start // 128
    row_of = iota((rows, 128), 0)
    owners, places = [], []
    for j in range(2):
        window = jnp.sum(jnp.where(row_of == first + j, order, 0), axis=0, keepdims=True)
        place = (first + j) * 128 + iota((1, 128), 1) - start
        real = (place >= 0) & (place < count)
        owners.append(jnp.where(real, window // own, -1))
        places.append(place)
    owner_hot = jnp.concatenate([iota((groups, 128), 0) == o for o in owners], axis=1)
    place_hot = jnp.concatenate([iota((slots, 128), 0) == p for p in places], axis=1)
    slot_of = dot(owner_hot.astype(BF16), place_hot.astype(BF16), NT).astype(BF16)
    obs_send[...] = dot(slot_of, obs_ref[...])

    local = order - me * own
    lane = iota((own, 128), 1)
    sub = iota((own, 128), 0)
    total = jnp.zeros((own, 128), jnp.int32)
    for r in range(rows):
        total = total + jnp.where(local[r : r + 1] == sub, lane + r * 128, 0)
    position = jnp.sum(total, axis=1, keepdims=True)
    batch_hot = ((position >= starts) & (position < ends)).astype(BF16)

    pl.semaphore_wait(barrier, groups + parts - 2)

    def to_group(src, dst, s):
        def send(k, carry):
            o = lax.rem(me + k, groups)
            pltpu.make_async_remote_copy(
                src_ref=src.at[pl.ds(o, 1)],
                dst_ref=dst.at[pl.ds(me, 1)],
                send_sem=gsem.at[s],
                recv_sem=gsem.at[s + 1],
                device_id=(o, x),
                device_id_type=MESH,
            ).start()
            return carry

        lax.fori_loop(1, groups, send, 0)
        dst[pl.ds(me, 1), :] = src[pl.ds(me, 1), :]

    def drain(ref, s):
        some = ref.at[pl.ds(0, groups - 1)]
        pltpu.make_async_copy(some, some, gsem.at[s]).wait()

    def to_parts(ref, s):
        copies = []
        for k in range(1, parts):
            copy = pltpu.make_async_remote_copy(
                src_ref=ref.at[x],
                dst_ref=ref.at[x],
                send_sem=xsem.at[s, 0, k],
                recv_sem=xsem.at[s, 1, k],
                device_id=(me, lax.rem(x + k, parts)),
                device_id_type=MESH,
            )
            copy.start()
            copies.append(copy)
        return copies

    to_group(obs_send, obs_recv, 0)
    hid_all[x] = hidden_ref[...]
    hid_copies = to_parts(hid_all, 0)
    for copy in hid_copies:
        copy.wait_recv()
    loads[0].wait()
    gates = jnp.zeros((own, 4 * units), F32)
    for p in range(parts):
        gates = gates + dot(hid_all[p], ws[p * units : (p + 1) * units])
    loads[1].wait()
    loads[2].wait()

    drain(obs_recv, 1)
    obs_all[x] = dot(batch_hot, obs_recv[...].astype(BF16)).astype(BF16)
    obs_copies = to_parts(obs_all, 1)
    for copy in obs_copies:
        copy.wait_recv()
    features = obs_ref.shape[1]
    for p in range(parts):
        gates = gates + dot(obs_all[p], wi[p * features : (p + 1) * features])
    gate = [
        gates[:, g * units : (g + 1) * units] + gate_bias_ref[g : g + 1, :] for g in range(4)
    ]
    cell = jax.nn.sigmoid(gate[1]) * cell_ref[...].astype(F32) + jax.nn.sigmoid(
        gate[0]
    ) * jnp.tanh(gate[2])
    hidden = (jax.nn.sigmoid(gate[3]) * jnp.tanh(cell)).astype(BF16)
    new_all[x] = hidden
    new_copies = to_parts(new_all, 2)
    hidden_out[...] = hidden
    cell_out[...] = cell.astype(BF16)
    for copy in new_copies:
        copy.wait_recv()
    stream = jnp.zeros((own, 2 * head_units), F32)
    for p in range(parts):
        stream = stream + dot(new_all[p], wh[p * units : (p + 1) * units])
    streams = [
        jnp.maximum(
            stream[:, i * head_units : (i + 1) * head_units] + head_bias_ref[i : i + 1, :], 0.0
        ).astype(BF16)
        for i in range(2)
    ]
    value = dot(streams[0], value_weight_ref[...])
    advantage = dot(streams[1], adv_weight_ref[...])
    part_all[x] = jnp.zeros((own, 128), F32)
    part_all[x, :, 0:actions] = (
        value + advantage - jnp.mean(advantage, axis=1, keepdims=True)
    )
    part_copies = to_parts(part_all, 3)
    for copy in part_copies:
        copy.wait_recv()
    bias = adv_bias_ref[...]
    bias = value_bias_ref[...] + bias - jnp.mean(bias, axis=1, keepdims=True)
    part_sum = part_all[0] + part_all[1] + part_all[2] + part_all[3]
    val_send[...] = jnp.zeros((groups, 128), F32)
    val_send[:, 0:actions] = pick(batch_hot, part_sum[:, 0:actions] + bias, TN)
    to_group(val_send, val_recv, 2)
    for copies in (hid_copies, obs_copies, new_copies, part_copies):
        for copy in copies:
            copy.wait_send()
    drain(obs_send, 0)
    drain(val_send, 2)
    drain(val_recv, 3)
    q_out[...] = pick(slot_of, val_recv[...], TN)[:, 0:actions]


def solution(mesh):
    groups, parts = mesh.shape["group"], mesh.shape["mp"]

    def per_device(
        observations,
        hidden_state,
        cell_state,
        arrival_order,
        batch_counts,
        input_weight,
        state_weight,
        gate_bias,
        head_weight,
        head_bias,
        value_weight,
        value_bias,
        advantage_weight,
        advantage_bias,
    ):
        slots, features = observations.shape
        own, units = hidden_state.shape
        head_units = head_bias.shape[1]
        actions = advantage_weight.shape[1]
        vmem = pl.BlockSpec(memory_space=pltpu.VMEM)
        hbm = pl.BlockSpec(memory_space=pl.ANY)
        dma = pltpu.SemaphoreType.DMA
        wi = input_weight.reshape(input_weight.shape[0], -1)
        ws = state_weight.reshape(state_weight.shape[0], -1)
        wh = head_weight.reshape(head_weight.shape[0], -1)
        return pl.pallas_call(
            functools.partial(step_kernel, groups, parts),
            name="acting_step",
            out_shape=(
                jax.ShapeDtypeStruct((slots, actions), F32),
                jax.ShapeDtypeStruct((own, units), BF16),
                jax.ShapeDtypeStruct((own, units), BF16),
            ),
            in_specs=[vmem] * 5 + [hbm, hbm, vmem, hbm] + [vmem] * 5,
            out_specs=(vmem,) * 3,
            scratch_shapes=[
                pltpu.VMEM(wi.shape, BF16),
                pltpu.VMEM(ws.shape, BF16),
                pltpu.VMEM(wh.shape, BF16),
                pltpu.VMEM((groups, features), F32),
                pltpu.VMEM((groups, features), F32),
                pltpu.VMEM((parts, own, features), BF16),
                pltpu.VMEM((parts, own, units), BF16),
                pltpu.VMEM((parts, own, units), BF16),
                pltpu.VMEM((parts, own, 128), F32),
                pltpu.VMEM((groups, 128), F32),
                pltpu.VMEM((groups, 128), F32),
                dma((3,)),
                dma((4,)),
                dma((4, 2, parts)),
            ],
            compiler_params=pltpu.CompilerParams(
                collective_id=0, has_side_effects=True, vmem_limit_bytes=32 * 2**20
            ),
        )(
            observations,
            hidden_state,
            cell_state,
            arrival_order.reshape(-1, 128),
            batch_counts.reshape(1, -1),
            wi,
            ws,
            gate_bias,
            wh,
            head_bias,
            value_weight,
            value_bias.reshape(1, 1),
            advantage_weight,
            advantage_bias.reshape(1, -1),
        )

    placed = (
        P("group", "mp"),
        P("group", "mp"),
        P("group", "mp"),
        P(),
        P(),
        P(None, None, "mp"),
        P(None, None, "mp"),
        P(None, "mp"),
        P(None, None, "mp"),
        P(None, "mp"),
        P("mp", None),
        P(),
        P("mp", None),
        P(),
    )
    return jax.shard_map(
        per_device,
        mesh=mesh,
        in_specs=placed,
        out_specs=(P("group", None), P("group", "mp"), P("group", "mp")),
        check_vma=False,
    )
```

```python
import functools

import jax
import jax.numpy as jnp
from jax import lax
from jax.experimental import pallas as pl
from jax.experimental.pallas import tpu as pltpu
from jax.sharding import PartitionSpec as P

MESH = pl.DeviceIdType.MESH
F32 = jnp.float32
BF16 = jnp.bfloat16
NT = (((1,), (1,)), ((), ()))


def iota(shape, dim):
    return lax.broadcasted_iota(jnp.int32, shape, dim)


NN = (((1,), (0,)), ((), ()))


def dot(a, b, dims=NN):
    return lax.dot_general(a, b, dims, preferred_element_type=F32)


def pick(table, values):
    high = values.astype(BF16)
    rest = values - high.astype(F32)
    mid = rest.astype(BF16)
    low = (rest - mid.astype(F32)).astype(BF16)
    return dot(table, high) + dot(table, mid) + dot(table, low)


def regroup(src, dst):
    gates = dst.shape[0]
    block = 16

    def body(i, carry):
        at = pl.multiple_of(i * block, block)
        v = src[pl.ds(at, block)].astype(F32)
        t = pltpu.einshape("kjn->jkn", v).astype(BF16)
        for j in range(v.shape[1]):
            half, g = divmod(j, gates)
            dst[g, pl.ds(at, block), half * 128 : half * 128 + 128] = t[j]
        return carry

    lax.fori_loop(0, src.shape[0] // block, body, 0, unroll=4)


def step_kernel(
    groups,
    parts,
    peers,
    obs_in,
    hidden_in,
    cell_in,
    order_in,
    counts_in,
    wi_in,
    ws_in,
    gate_bias_in,
    wh_in,
    head_bias_in,
    value_weight_in,
    value_bias_in,
    adv_weight_in,
    adv_bias_in,
    q_out,
    hidden_out,
    cell_out,
    obs_ref,
    cell_ref,
    order_ref,
    counts_ref,
    gate_bias_ref,
    head_bias_ref,
    value_weight_ref,
    value_bias_ref,
    adv_weight_ref,
    adv_bias_ref,
    wi_raw,
    ws_raw,
    wh_raw,
    wi,
    ws,
    wh,
    obs_send,
    obs_recv,
    obs_all,
    hid_all,
    new_all,
    part_all,
    val_send,
    val_recv,
    batch_t,
    slot_t,
    lsem,
    gsem,
    xsem,
):
    me = lax.axis_index("group")
    x = lax.axis_index("mp")
    own = hidden_in.shape[0]
    slots = obs_ref.shape[0]
    features = obs_ref.shape[1]
    units = cell_ref.shape[1]
    head_units = head_bias_ref.shape[1]
    actions = adv_weight_ref.shape[0]

    loads = [
        pltpu.make_async_copy(src, dst, lsem.at[i])
        for i, (src, dst) in enumerate(
            (
                (order_in, order_ref),
                (counts_in, counts_ref),
                (obs_in, obs_ref),
                (ws_in, ws_raw),
                (hidden_in, hid_all.at[x]),
                (wi_in, wi_raw),
                (wh_in, wh_raw),
                (cell_in, cell_ref),
                (gate_bias_in, gate_bias_ref),
                (head_bias_in, head_bias_ref),
                (value_weight_in, value_weight_ref),
                (value_bias_in, value_bias_ref),
                (adv_weight_in, adv_weight_ref),
                (adv_bias_in, adv_bias_ref),
            )
        )
    ]
    for load in loads[:3]:
        load.start()
    barrier = pltpu.get_barrier_semaphore()
    others = [peer(me) for peer in peers]
    for other in others:
        pl.semaphore_signal(barrier, inc=1, device_id=(other, x), device_id_type=MESH)
    for k in range(1, parts):
        pl.semaphore_signal(
            barrier, inc=1, device_id=(me, lax.rem(x + k, parts)), device_id_type=MESH
        )
    for load in loads[3:]:
        load.start()

    loads[0].wait()
    loads[1].wait()
    counts = jnp.broadcast_to(counts_ref[...], (8, groups))
    before = (iota((groups, groups), 0) < iota((groups, groups), 1)).astype(BF16)
    starts = dot(counts.astype(BF16), before).astype(jnp.int32)[0:1]
    ends = starts + counts[0:1]
    mine = iota((1, groups), 1) == me
    start = jnp.sum(jnp.where(mine, starts, 0), axis=1, keepdims=True)
    count = jnp.sum(jnp.where(mine, counts[0:1], 0), axis=1, keepdims=True)
    order = order_ref[...]
    rows = order.shape[0]
    first = start // 128
    row_of = iota((rows, 128), 0)
    owners, places = [], []
    for j in range(2):
        window = jnp.sum(jnp.where(row_of == first + j, order, 0), axis=0, keepdims=True)
        place = (first + j) * 128 + iota((1, 128), 1) - start
        real = (place >= 0) & (place < count)
        owners.append(jnp.where(real, window // own, -1))
        places.append(place)
    owner_hot = jnp.concatenate([iota((groups, 128), 0) == o for o in owners], axis=1)
    place_hot = jnp.concatenate([iota((slots, 128), 0) == p for p in places], axis=1)
    owner_hot = owner_hot.astype(BF16)
    place_hot = place_hot.astype(BF16)
    slot_of = dot(owner_hot, place_hot, NT).astype(BF16)
    slot_t[...] = dot(place_hot, owner_hot, NT).astype(BF16)
    loads[2].wait()
    obs_send[...] = dot(slot_of, obs_ref[...])

    local = order - me * own
    lane = iota((own, 128), 1)
    sub = iota((own, 128), 0)
    total = jnp.zeros((own, 128), jnp.int32)
    for r in range(rows):
        total = total + jnp.where(local[r : r + 1] == sub, lane + r * 128, 0)
    position = jnp.sum(total, axis=1, keepdims=True)
    batch_hot = ((position >= starts) & (position < ends)).astype(F32)
    batch_t[...] = batch_hot.T.astype(BF16)
    batch_hot = batch_hot.astype(BF16)

    loads[3].wait()
    regroup(ws_raw, ws)

    pl.semaphore_wait(barrier, groups + parts - 2)

    def to_group(src, dst, s):
        for other in others:
            pltpu.make_async_remote_copy(
                src_ref=src.at[pl.ds(other, 1)],
                dst_ref=dst.at[pl.ds(me, 1)],
                send_sem=gsem.at[s],
                recv_sem=gsem.at[s + 1],
                device_id=(other, x),
                device_id_type=MESH,
            ).start()
        dst[pl.ds(me, 1), :] = src[pl.ds(me, 1), :]

    def drain(ref, s):
        some = ref.at[pl.ds(0, groups - 1)]
        pltpu.make_async_copy(some, some, gsem.at[s]).wait()

    def to_parts(ref, s):
        copies = []
        for k in (2, 1, 3):
            copy = pltpu.make_async_remote_copy(
                src_ref=ref.at[x],
                dst_ref=ref.at[x],
                send_sem=xsem.at[s, 0, k],
                recv_sem=xsem.at[s, 1, k],
                device_id=(me, lax.rem(x + k, parts)),
                device_id_type=MESH,
            )
            copy.start()
            copies.append(copy)
        return copies

    def over_parts(ref, copies, add):
        add(x, ref[x])
        for copy, k in zip(copies[1:] + copies[:1], (3, 1, 2)):
            copy.wait_recv()
            p = lax.rem(x + k, parts)
            add(p, ref[p])

    to_group(obs_send, obs_recv, 0)
    loads[4].wait()
    hid_copies = to_parts(hid_all, 0)
    loads[5].wait()
    regroup(wi_raw, wi)
    loads[6].wait()
    for i in range(2):
        wh[i] = wh_raw[:, i, :]
    for load in loads[7:]:
        load.wait()
    gate = [jnp.broadcast_to(gate_bias_ref[g : g + 1, :], (own, units)) for g in range(4)]

    def add_state(p, block):
        at = pl.ds(pl.multiple_of(p * units, units), units)
        for g in range(4):
            gate[g] = gate[g] + dot(block, ws[g, at, :])

    over_parts(hid_all, hid_copies, add_state)
    bias = adv_bias_ref[...]
    bias = value_bias_ref[...].reshape(1, 1) + bias - jnp.mean(bias, axis=1, keepdims=True)

    drain(obs_recv, 1)
    obs_all[x] = dot(batch_hot, obs_recv[...].astype(BF16)).astype(BF16)
    obs_copies = to_parts(obs_all, 1)

    def add_input(p, block):
        at = pl.ds(pl.multiple_of(p * features, features), features)
        for g in range(4):
            gate[g] = gate[g] + dot(block, wi[g, at, :])

    over_parts(obs_all, obs_copies, add_input)
    cell = jax.nn.sigmoid(gate[1]) * cell_ref[...].astype(F32) + jax.nn.sigmoid(
        gate[0]
    ) * jnp.tanh(gate[2])
    hidden = (jax.nn.sigmoid(gate[3]) * jnp.tanh(cell)).astype(BF16)
    new_all[x] = hidden
    new_copies = to_parts(new_all, 2)
    hidden_out[...] = hidden
    cell_out[...] = cell.astype(BF16)
    stream = [jnp.broadcast_to(head_bias_ref[i : i + 1, :], (own, head_units)) for i in range(2)]

    def add_head(p, block):
        at = pl.ds(pl.multiple_of(p * units, units), units)
        for i in range(2):
            stream[i] = stream[i] + dot(block, wh[i, at, :])

    over_parts(new_all, new_copies, add_head)
    stream = [jnp.maximum(s, 0.0).astype(BF16) for s in stream]
    value = jnp.sum(
        stream[0].astype(F32) * value_weight_ref[...].astype(F32), axis=1, keepdims=True
    )
    advantage = dot(stream[1], adv_weight_ref[...], NT)
    part_all[x] = jnp.zeros((own, 128), F32)
    part_all[x, :, 0:actions] = (
        value + advantage - jnp.mean(advantage, axis=1, keepdims=True)
    )
    part_copies = to_parts(part_all, 3)
    val_send[...] = jnp.zeros((groups, 128), F32)
    for copy in part_copies:
        copy.wait_recv()
    part_sum = part_all[0] + part_all[1] + part_all[2] + part_all[3]
    val_send[:, 0:actions] = pick(batch_t[...], part_sum[:, 0:actions] + bias)
    to_group(val_send, val_recv, 2)
    for copies in (hid_copies, obs_copies, new_copies, part_copies):
        for copy in copies:
            copy.wait_send()
    drain(obs_send, 0)
    drain(val_send, 2)
    drain(val_recv, 3)
    q_out[...] = pick(slot_t[...], val_recv[...])


def out_kernel(q_ref, hidden_ref, cell_ref, q_out, hidden_out, cell_out):
    hidden_out[...] = hidden_ref[...]
    cell_out[...] = cell_ref[...]
    q_out[...] = q_ref[...].T[0 : q_out.shape[0]]


def farthest_first(groups):
    side = 8
    ring = lambda d: min(d, side - d)
    moves = [(dz, dy, dc) for dz in range(side) for dy in range(side) for dc in range(2)]
    moves.sort(key=lambda m: -10 * (ring(m[0]) + ring(m[1])) - m[2])

    def peer(dz, dy, dc):
        def index(me):
            z, y, c = me // (2 * side), lax.rem(me // 2, side), lax.rem(me, 2)
            z, y, c = lax.rem(z + dz, side), lax.rem(y + dy, side), lax.rem(c + dc, 2)
            return (z * side + y) * 2 + c

        return index

    assert len(moves) == groups
    return [peer(*m) for m in moves if any(m)]


def solution(mesh):
    groups, parts = mesh.shape["group"], mesh.shape["mp"]

    def per_device(
        observations,
        hidden_state,
        cell_state,
        arrival_order,
        batch_counts,
        input_weight,
        state_weight,
        gate_bias,
        head_weight,
        head_bias,
        value_weight,
        value_bias,
        advantage_weight,
        advantage_bias,
    ):
        slots, features = observations.shape
        own, units = hidden_state.shape
        head_units = head_bias.shape[1]
        actions = advantage_weight.shape[1]
        vmem = pl.BlockSpec(memory_space=pltpu.VMEM)
        hbm = pl.BlockSpec(memory_space=pltpu.HBM)
        dma = pltpu.SemaphoreType.DMA

        def as_stored(w):
            return w.reshape(-1, 4, 2, 128).transpose(0, 2, 1, 3).reshape(-1, 8, 128)

        wi, ws = as_stored(input_weight), as_stored(state_weight)
        order = arrival_order.reshape(-1, 128)
        counts = batch_counts.reshape(1, -1)
        vw, aw, ab = value_weight.T, advantage_weight.T, advantage_bias.reshape(1, -1)
        like = lambda a: pltpu.VMEM(a.shape, a.dtype)
        q, new_hidden, new_cell = pl.pallas_call(
            functools.partial(step_kernel, groups, parts, farthest_first(groups)),
            name="acting_step",
            out_shape=(
                jax.ShapeDtypeStruct((slots, 128), F32),
                jax.ShapeDtypeStruct((own, units), BF16),
                jax.ShapeDtypeStruct((own, units), BF16),
            ),
            in_specs=[hbm] * 14,
            out_specs=(vmem,) * 3,
            scratch_shapes=[
                like(observations),
                like(cell_state),
                like(order),
                like(counts),
                like(gate_bias),
                like(head_bias),
                like(vw),
                like(value_bias),
                like(aw),
                like(ab),
                like(wi),
                like(ws),
                like(head_weight),
                pltpu.VMEM((4, wi.shape[0], units), BF16),
                pltpu.VMEM((4, ws.shape[0], units), BF16),
                pltpu.VMEM((2, head_weight.shape[0], head_units), BF16),
                pltpu.VMEM((groups, features), F32),
                pltpu.VMEM((groups, features), F32),
                pltpu.VMEM((parts, own, features), BF16),
                pltpu.VMEM((parts, own, units), BF16),
                pltpu.VMEM((parts, own, units), BF16),
                pltpu.VMEM((parts, own, 128), F32),
                pltpu.VMEM((groups, 128), F32),
                pltpu.VMEM((groups, 128), F32),
                pltpu.VMEM((groups, own), BF16),
                pltpu.VMEM((slots, groups), BF16),
                dma((14,)),
                dma((4,)),
                dma((4, 2, parts)),
            ],
            compiler_params=pltpu.CompilerParams(
                collective_id=0, has_side_effects=True, vmem_limit_bytes=60000000
            ),
        )(
            observations,
            hidden_state,
            cell_state,
            order,
            counts,
            wi,
            ws,
            gate_bias,
            head_weight,
            head_bias,
            vw,
            value_bias,
            aw,
            ab,
        )
        q, new_hidden, new_cell = pl.pallas_call(
            out_kernel,
            name="outputs",
            out_shape=(
                jax.ShapeDtypeStruct((actions, slots), F32),
                jax.ShapeDtypeStruct((own, units), BF16),
                jax.ShapeDtypeStruct((own, units), BF16),
            ),
            in_specs=[vmem] * 3,
            out_specs=(vmem,) * 3,
            compiler_params=pltpu.CompilerParams(vmem_limit_bytes=4 * 2**20),
        )(q, new_hidden, new_cell)
        return q.T, new_hidden, new_cell

    placed = (
        P("group", "mp"),
        P("group", "mp"),
        P("group", "mp"),
        P(),
        P(),
        P(None, None, "mp"),
        P(None, None, "mp"),
        P(None, "mp"),
        P(None, None, "mp"),
        P(None, "mp"),
        P("mp", None),
        P(),
        P("mp", None),
        P(),
    )
    return jax.shard_map(
        per_device,
        mesh=mesh,
        in_specs=placed,
        out_specs=(P("group", None), P("group", "mp"), P("group", "mp")),
        check_vma=False,
    )
```

```python
import functools

import jax
import jax.numpy as jnp
from jax import lax
from jax.experimental import pallas as pl
from jax.experimental.pallas import tpu as pltpu
from jax.sharding import PartitionSpec as P

MESH = pl.DeviceIdType.MESH
F32 = jnp.float32
BF16 = jnp.bfloat16
NT = (((1,), (1,)), ((), ()))


def iota(shape, dim):
    return lax.broadcasted_iota(jnp.int32, shape, dim)


NN = (((1,), (0,)), ((), ()))


def dot(a, b, dims=NN):
    return lax.dot_general(a, b, dims, preferred_element_type=F32)


def pick(table, values):
    high = values.astype(BF16)
    rest = values - high.astype(F32)
    mid = rest.astype(BF16)
    low = (rest - mid.astype(F32)).astype(BF16)
    return dot(table, high) + dot(table, mid) + dot(table, low)


def regroup(src, dst):
    gates = dst.shape[0]
    block = 16

    def body(i, carry):
        at = pl.multiple_of(i * block, block)
        v = src[pl.ds(at, block)].astype(F32)
        t = pltpu.einshape("kjn->jkn", v).astype(BF16)
        for j in range(v.shape[1]):
            half, g = divmod(j, gates)
            dst[g, pl.ds(at, block), half * 128 : half * 128 + 128] = t[j]
        return carry

    lax.fori_loop(0, src.shape[0] // block, body, 0, unroll=4)


def step_kernel(
    groups,
    parts,
    peers,
    obs_in,
    hidden_in,
    cell_in,
    order_in,
    counts_in,
    wi_in,
    ws_in,
    gate_bias_in,
    wh_in,
    head_bias_in,
    value_weight_in,
    value_bias_ref,
    adv_weight_in,
    adv_bias_in,
    q_out,
    hidden_out,
    cell_out,
    obs_ref,
    cell_ref,
    order_ref,
    counts_ref,
    gate_bias_ref,
    head_bias_ref,
    value_weight_ref,
    adv_weight_ref,
    adv_bias_ref,
    wi_raw,
    ws_raw,
    wh_raw,
    wi,
    ws,
    wh,
    obs_send,
    obs_recv,
    obs_all,
    hid_all,
    new_all,
    part_all,
    val_send,
    val_recv,
    batch_t,
    slot_t,
    lsem,
    gsem,
    xsem,
):
    me = lax.axis_index("group")
    x = lax.axis_index("mp")
    own = hidden_in.shape[0]
    slots = obs_ref.shape[0]
    features = obs_ref.shape[1]
    units = cell_ref.shape[1]
    head_units = head_bias_ref.shape[1]
    actions = adv_weight_ref.shape[0]

    loads = [
        pltpu.make_async_copy(src, dst, lsem.at[i])
        for i, (src, dst) in enumerate(
            (
                (order_in, order_ref),
                (counts_in, counts_ref),
                (obs_in, obs_ref),
                (ws_in, ws_raw),
                (hidden_in, hid_all.at[x]),
                (wi_in, wi_raw),
                (wh_in, wh_raw),
                (cell_in, cell_ref),
                (gate_bias_in, gate_bias_ref),
                (head_bias_in, head_bias_ref),
                (value_weight_in, value_weight_ref),
                (adv_weight_in, adv_weight_ref),
                (adv_bias_in, adv_bias_ref),
            )
        )
    ]
    for load in loads[:3]:
        load.start()
    barrier = pltpu.get_barrier_semaphore()
    others = [peer(me) for peer in peers]
    for other in others:
        pl.semaphore_signal(barrier, inc=1, device_id=(other, x), device_id_type=MESH)
    for k in range(1, parts):
        pl.semaphore_signal(
            barrier, inc=1, device_id=(me, lax.rem(x + k, parts)), device_id_type=MESH
        )
    for load in loads[3:]:
        load.start()

    loads[0].wait()
    loads[1].wait()
    counts = jnp.broadcast_to(counts_ref[...], (8, groups))
    before = (iota((groups, groups), 0) < iota((groups, groups), 1)).astype(BF16)
    starts = dot(counts.astype(BF16), before).astype(jnp.int32)[0:1]
    ends = starts + counts[0:1]
    mine = iota((1, groups), 1) == me
    start = jnp.sum(jnp.where(mine, starts, 0), axis=1, keepdims=True)
    count = jnp.sum(jnp.where(mine, counts[0:1], 0), axis=1, keepdims=True)
    order = order_ref[...]
    rows = order.shape[0]
    first = start // 128
    row_of = iota((rows, 128), 0)
    owners, places = [], []
    for j in range(2):
        window = jnp.sum(jnp.where(row_of == first + j, order, 0), axis=0, keepdims=True)
        place = (first + j) * 128 + iota((1, 128), 1) - start
        real = (place >= 0) & (place < count)
        owners.append(jnp.where(real, window // own, -1))
        places.append(place)
    owner_hot = jnp.concatenate([iota((groups, 128), 0) == o for o in owners], axis=1)
    place_hot = jnp.concatenate([iota((slots, 128), 0) == p for p in places], axis=1)
    owner_hot = owner_hot.astype(BF16)
    place_hot = place_hot.astype(BF16)
    slot_of = dot(owner_hot, place_hot, NT).astype(BF16)
    slot_t[...] = dot(place_hot, owner_hot, NT).astype(BF16)
    loads[2].wait()
    obs_send[...] = dot(slot_of, obs_ref[...])

    local = order - me * own
    lane = iota((own, 128), 1)
    sub = iota((own, 128), 0)
    total = jnp.zeros((own, 128), jnp.int32)
    for r in range(rows):
        total = total + jnp.where(local[r : r + 1] == sub, lane + r * 128, 0)
    position = jnp.sum(total, axis=1, keepdims=True)
    batch_hot = ((position >= starts) & (position < ends)).astype(F32)
    batch_t[...] = batch_hot.T.astype(BF16)
    batch_hot = batch_hot.astype(BF16)

    pl.semaphore_wait(barrier, groups + parts - 2)

    def to_group(src, dst, s):
        for other in others:
            pltpu.make_async_remote_copy(
                src_ref=src.at[pl.ds(other, 1)],
                dst_ref=dst.at[pl.ds(me, 1)],
                send_sem=gsem.at[s],
                recv_sem=gsem.at[s + 1],
                device_id=(other, x),
                device_id_type=MESH,
            ).start()
        dst[pl.ds(me, 1), :] = src[pl.ds(me, 1), :]

    def drain(ref, s):
        some = ref.at[pl.ds(0, groups - 1)]
        pltpu.make_async_copy(some, some, gsem.at[s]).wait()

    def to_parts(ref, s):
        copies = []
        for k in (2, 1, 3):
            copy = pltpu.make_async_remote_copy(
                src_ref=ref.at[x],
                dst_ref=ref.at[x],
                send_sem=xsem.at[s, 0, k],
                recv_sem=xsem.at[s, 1, k],
                device_id=(me, lax.rem(x + k, parts)),
                device_id_type=MESH,
            )
            copy.start()
            copies.append(copy)
        return copies

    def over_parts(ref, copies, add):
        add(x, ref[x])
        for copy, k in zip(copies[1:] + copies[:1], (3, 1, 2)):
            copy.wait_recv()
            p = lax.rem(x + k, parts)
            add(p, ref[p])

    to_group(obs_send, obs_recv, 0)
    loads[4].wait()
    hid_copies = to_parts(hid_all, 0)
    loads[5].wait()
    regroup(wi_raw, wi)
    loads[3].wait()
    regroup(ws_raw, ws)
    loads[6].wait()
    for i in range(2):
        wh[i] = wh_raw[:, i, :]
    for load in loads[7:]:
        load.wait()
    gate = [jnp.broadcast_to(gate_bias_ref[g : g + 1, :], (own, units)) for g in range(4)]

    def add_state(p, block):
        at = pl.ds(pl.multiple_of(p * units, units), units)
        for g in range(4):
            gate[g] = gate[g] + dot(block, ws[g, at, :])

    over_parts(hid_all, hid_copies, add_state)
    bias = adv_bias_ref[...]
    bias = value_bias_ref[0] + bias - jnp.mean(bias, axis=1, keepdims=True)

    drain(obs_recv, 1)
    obs_all[x] = dot(batch_hot, obs_recv[...].astype(BF16)).astype(BF16)
    obs_copies = to_parts(obs_all, 1)

    def add_input(p, block):
        at = pl.ds(pl.multiple_of(p * features, features), features)
        for g in range(4):
            gate[g] = gate[g] + dot(block, wi[g, at, :])

    over_parts(obs_all, obs_copies, add_input)
    cell = jax.nn.sigmoid(gate[1]) * cell_ref[...].astype(F32) + jax.nn.sigmoid(
        gate[0]
    ) * jnp.tanh(gate[2])
    hidden = (jax.nn.sigmoid(gate[3]) * jnp.tanh(cell)).astype(BF16)
    new_all[x] = hidden
    new_copies = to_parts(new_all, 2)
    hidden_out[...] = hidden
    cell_out[...] = cell.astype(BF16)
    stream = [jnp.broadcast_to(head_bias_ref[i : i + 1, :], (own, head_units)) for i in range(2)]

    def add_head(p, block):
        at = pl.ds(pl.multiple_of(p * units, units), units)
        for i in range(2):
            stream[i] = stream[i] + dot(block, wh[i, at, :])

    over_parts(new_all, new_copies, add_head)
    stream = [jnp.maximum(s, 0.0).astype(BF16) for s in stream]
    value = jnp.sum(
        stream[0].astype(F32) * value_weight_ref[...].astype(F32), axis=1, keepdims=True
    )
    advantage = dot(stream[1], adv_weight_ref[...], NT)
    part_all[x] = jnp.zeros((own, 128), F32)
    part_all[x, :, 0:actions] = (
        value + advantage - jnp.mean(advantage, axis=1, keepdims=True)
    )
    part_copies = to_parts(part_all, 3)
    val_send[...] = jnp.zeros((groups, 128), F32)
    for copy in part_copies:
        copy.wait_recv()
    part_sum = part_all[0] + part_all[1] + part_all[2] + part_all[3]
    val_send[:, 0:actions] = pick(batch_t[...], part_sum[:, 0:actions] + bias)
    to_group(val_send, val_recv, 2)
    for copies in (hid_copies, obs_copies, new_copies, part_copies):
        for copy in copies:
            copy.wait_send()
    drain(obs_send, 0)
    drain(val_send, 2)
    drain(val_recv, 3)
    q_out[...] = pick(slot_t[...], val_recv[...])


def out_kernel(q_ref, hidden_ref, cell_ref, q_out, hidden_out, cell_out):
    hidden_out[...] = hidden_ref[...]
    cell_out[...] = cell_ref[...]
    q_out[...] = q_ref[...].T[0 : q_out.shape[0]]


def farthest_first(groups):
    side = 8
    ring = lambda d: min(d, side - d)
    moves = [(dz, dy, dc) for dz in range(side) for dy in range(side) for dc in range(2)]
    moves.sort(key=lambda m: -10 * (ring(m[0]) + ring(m[1])) - m[2])

    def peer(dz, dy, dc):
        def index(me):
            z, y, c = me // (2 * side), lax.rem(me // 2, side), lax.rem(me, 2)
            z, y, c = lax.rem(z + dz, side), lax.rem(y + dy, side), lax.rem(c + dc, 2)
            return (z * side + y) * 2 + c

        return index

    assert len(moves) == groups
    return [peer(*m) for m in moves if any(m)]


def solution(mesh):
    groups, parts = mesh.shape["group"], mesh.shape["mp"]

    def per_device(
        observations,
        hidden_state,
        cell_state,
        arrival_order,
        batch_counts,
        input_weight,
        state_weight,
        gate_bias,
        head_weight,
        head_bias,
        value_weight,
        value_bias,
        advantage_weight,
        advantage_bias,
    ):
        slots, features = observations.shape
        own, units = hidden_state.shape
        head_units = head_bias.shape[1]
        actions = advantage_weight.shape[1]
        vmem = pl.BlockSpec(memory_space=pltpu.VMEM)
        smem = pl.BlockSpec(memory_space=pltpu.SMEM)
        hbm = pl.BlockSpec(memory_space=pltpu.HBM)
        dma = pltpu.SemaphoreType.DMA

        def as_stored(w):
            return w.reshape(-1, 4, 2, 128).transpose(0, 2, 1, 3).reshape(-1, 8, 128)

        wi, ws = as_stored(input_weight), as_stored(state_weight)
        order = arrival_order.reshape(-1, 128)
        counts = batch_counts.reshape(1, -1)
        vw, aw, ab = value_weight.T, advantage_weight.T, advantage_bias.reshape(1, -1)
        like = lambda a: pltpu.VMEM(a.shape, a.dtype)
        q, new_hidden, new_cell = pl.pallas_call(
            functools.partial(step_kernel, groups, parts, farthest_first(groups)),
            name="acting_step",
            out_shape=(
                jax.ShapeDtypeStruct((slots, 128), F32),
                jax.ShapeDtypeStruct((own, units), BF16),
                jax.ShapeDtypeStruct((own, units), BF16),
            ),
            in_specs=[hbm] * 11 + [smem] + [hbm] * 2,
            out_specs=(vmem,) * 3,
            scratch_shapes=[
                like(observations),
                like(cell_state),
                like(order),
                like(counts),
                like(gate_bias),
                like(head_bias),
                like(vw),
                like(aw),
                like(ab),
                like(wi),
                like(ws),
                like(head_weight),
                pltpu.VMEM((4, wi.shape[0], units), BF16),
                pltpu.VMEM((4, ws.shape[0], units), BF16),
                pltpu.VMEM((2, head_weight.shape[0], head_units), BF16),
                pltpu.VMEM((groups, features), F32),
                pltpu.VMEM((groups, features), F32),
                pltpu.VMEM((parts, own, features), BF16),
                pltpu.VMEM((parts, own, units), BF16),
                pltpu.VMEM((parts, own, units), BF16),
                pltpu.VMEM((parts, own, 128), F32),
                pltpu.VMEM((groups, 128), F32),
                pltpu.VMEM((groups, 128), F32),
                pltpu.VMEM((groups, own), BF16),
                pltpu.VMEM((slots, groups), BF16),
                dma((13,)),
                dma((4,)),
                dma((4, 2, parts)),
            ],
            compiler_params=pltpu.CompilerParams(
                collective_id=0, has_side_effects=True, vmem_limit_bytes=32 * 2**20
            ),
        )(
            *(
                a if a is value_bias else pltpu.with_memory_space_constraint(a, pltpu.HBM)
                for a in (
                    observations,
                    hidden_state,
                    cell_state,
                    order,
                    counts,
                    wi,
                    ws,
                    gate_bias,
                    head_weight,
                    head_bias,
                    vw,
                    value_bias,
                    aw,
                    ab,
                )
            )
        )
        q, new_hidden, new_cell = pl.pallas_call(
            out_kernel,
            name="outputs",
            out_shape=(
                jax.ShapeDtypeStruct((actions, slots), F32),
                jax.ShapeDtypeStruct((own, units), BF16),
                jax.ShapeDtypeStruct((own, units), BF16),
            ),
            in_specs=[vmem] * 3,
            out_specs=(vmem,) * 3,
            compiler_params=pltpu.CompilerParams(vmem_limit_bytes=4 * 2**20),
        )(q, new_hidden, new_cell)
        return q.T, new_hidden, new_cell

    placed = (
        P("group", "mp"),
        P("group", "mp"),
        P("group", "mp"),
        P(),
        P(),
        P(None, None, "mp"),
        P(None, None, "mp"),
        P(None, "mp"),
        P(None, None, "mp"),
        P(None, "mp"),
        P("mp", None),
        P(),
        P("mp", None),
        P(),
    )
    return jax.shard_map(
        per_device,
        mesh=mesh,
        in_specs=placed,
        out_specs=(P("group", None), P("group", "mp"), P("group", "mp")),
        check_vma=False,
    )
```

```python
import functools

import jax
import jax.numpy as jnp
from jax import lax
from jax.experimental import pallas as pl
from jax.experimental.pallas import tpu as pltpu
from jax.sharding import PartitionSpec as P

MESH = pl.DeviceIdType.MESH
F32 = jnp.float32
BF16 = jnp.bfloat16
NT = (((1,), (1,)), ((), ()))


def iota(shape, dim):
    return lax.broadcasted_iota(jnp.int32, shape, dim)


NN = (((1,), (0,)), ((), ()))


def dot(a, b, dims=NN):
    return lax.dot_general(a, b, dims, preferred_element_type=F32)


def pick(table, values):
    high = values.astype(BF16)
    rest = values - high.astype(F32)
    mid = rest.astype(BF16)
    low = (rest - mid.astype(F32)).astype(BF16)
    return dot(table, high) + dot(table, mid) + dot(table, low)


def regroup(src, dst):
    gates = dst.shape[0]
    block = 16

    def body(i, carry):
        at = pl.multiple_of(i * block, block)
        v = src[pl.ds(at, block)].astype(F32)
        t = pltpu.einshape("kjn->jkn", v).astype(BF16)
        for j in range(v.shape[1]):
            half, g = divmod(j, gates)
            dst[g, pl.ds(at, block), half * 128 : half * 128 + 128] = t[j]
        return carry

    lax.fori_loop(0, src.shape[0] // block, body, 0, unroll=4)


def step_kernel(
    groups,
    parts,
    peers,
    obs_in,
    hidden_in,
    cell_in,
    order_in,
    counts_in,
    wi_in,
    ws_in,
    gate_bias_in,
    wh_in,
    head_bias_in,
    value_weight_in,
    value_bias_ref,
    adv_weight_in,
    adv_bias_in,
    q_out,
    hidden_out,
    cell_out,
    obs_ref,
    cell_ref,
    order_ref,
    counts_ref,
    gate_bias_ref,
    head_bias_all,
    value_weight_all,
    adv_weight_all,
    adv_bias_ref,
    wi_raw,
    ws_raw,
    wh_raw,
    wi,
    ws,
    wh,
    obs_send,
    obs_recv,
    obs_all,
    hid_all,
    new_all,
    val_send,
    val_recv,
    batch_t,
    slot_t,
    lsem,
    gsem,
    xsem,
    ssem,
    bsem,
    fsem,
):
    me = lax.axis_index("group")
    x = lax.axis_index("mp")
    own = hidden_in.shape[0]
    slots = obs_ref.shape[0]
    features = obs_ref.shape[1]
    units = cell_ref.shape[1]
    head_units = head_bias_all.shape[2]
    actions = adv_weight_all.shape[1]
    core = lax.rem(me, 2)
    sibling = me + 1 - 2 * core
    half = wh_in.shape[0] // 2

    loads = [
        pltpu.make_async_copy(src, dst, lsem.at[i])
        for i, (src, dst) in enumerate(
            (
                (order_in, order_ref),
                (counts_in, counts_ref),
                (obs_in, obs_ref),
                (ws_in, ws_raw),
                (hidden_in, hid_all.at[x]),
                (wi_in, wi_raw),
                (wh_in, wh_raw),
                (cell_in, cell_ref),
                (gate_bias_in, gate_bias_ref),
                (head_bias_in, head_bias_all.at[x]),
                (value_weight_in, value_weight_all.at[x]),
                (adv_weight_in, adv_weight_all.at[x]),
                (adv_bias_in, adv_bias_ref),
            )
        )
    ]
    for load in loads[:3]:
        load.start()
    barrier = pltpu.get_barrier_semaphore()
    others = [peer(me) for peer in peers]
    for other in others:
        pl.semaphore_signal(barrier, inc=1, device_id=(other, x), device_id_type=MESH)
    for k in range(1, parts):
        pl.semaphore_signal(
            barrier, inc=1, device_id=(me, lax.rem(x + k, parts)), device_id_type=MESH
        )
    for load in loads[3:]:
        load.start()

    loads[0].wait()
    loads[1].wait()
    counts = jnp.broadcast_to(counts_ref[...], (8, groups))
    before = (iota((groups, groups), 0) < iota((groups, groups), 1)).astype(BF16)
    starts = dot(counts.astype(BF16), before).astype(jnp.int32)[0:1]
    ends = starts + counts[0:1]
    mine = iota((1, groups), 1) == me
    start = jnp.sum(jnp.where(mine, starts, 0), axis=1, keepdims=True)
    count = jnp.sum(jnp.where(mine, counts[0:1], 0), axis=1, keepdims=True)
    order = order_ref[...]
    rows = order.shape[0]
    first = start // 128
    row_of = iota((rows, 128), 0)
    owners, places = [], []
    for j in range(2):
        window = jnp.sum(jnp.where(row_of == first + j, order, 0), axis=0, keepdims=True)
        place = (first + j) * 128 + iota((1, 128), 1) - start
        real = (place >= 0) & (place < count)
        owners.append(jnp.where(real, window // own, -1))
        places.append(place)
    owner_hot = jnp.concatenate([iota((groups, 128), 0) == o for o in owners], axis=1)
    place_hot = jnp.concatenate([iota((slots, 128), 0) == p for p in places], axis=1)
    owner_hot = owner_hot.astype(BF16)
    place_hot = place_hot.astype(BF16)
    slot_of = dot(owner_hot, place_hot, NT).astype(BF16)
    slot_t[...] = dot(place_hot, owner_hot, NT).astype(BF16)
    loads[2].wait()
    obs_send[...] = dot(slot_of, obs_ref[...])

    local = order - me * own
    lane = iota((own, 128), 1)
    sub = iota((own, 128), 0)
    total = jnp.zeros((own, 128), jnp.int32)
    for r in range(rows):
        total = total + jnp.where(local[r : r + 1] == sub, lane + r * 128, 0)
    position = jnp.sum(total, axis=1, keepdims=True)
    batch_hot = ((position >= starts) & (position < ends)).astype(F32)
    batch_t[...] = batch_hot.T.astype(BF16)
    batch_hot = batch_hot.astype(BF16)

    loads[6].wait()
    for i in range(2):
        wh[x, i] = wh_raw[:, i, :]
    pl.semaphore_wait(barrier, groups + parts - 2)

    def to_group(src, dst, s):
        for other in others:
            pltpu.make_async_remote_copy(
                src_ref=src.at[pl.ds(other, 1)],
                dst_ref=dst.at[pl.ds(me, 1)],
                send_sem=gsem.at[s],
                recv_sem=gsem.at[s + 1],
                device_id=(other, x),
                device_id_type=MESH,
            ).start()
        dst[pl.ds(me, 1), :] = src[pl.ds(me, 1), :]

    def drain(ref, s):
        some = ref.at[pl.ds(0, groups - 1)]
        pltpu.make_async_copy(some, some, gsem.at[s]).wait()

    def to_parts(ref, s):
        copies = []
        for k in (2, 1, 3):
            copy = pltpu.make_async_remote_copy(
                src_ref=ref.at[x],
                dst_ref=ref.at[x],
                send_sem=xsem.at[s, 0, k],
                recv_sem=xsem.at[s, 1, k],
                device_id=(me, lax.rem(x + k, parts)),
                device_id_type=MESH,
            )
            copy.start()
            copies.append(copy)
        return copies

    def rows_at(first, count):
        return pl.ds(pl.multiple_of(core * half + first, count), count)

    whole = rows_at(0, half)
    quarters = {1: rows_at(0, half // 2), 3: rows_at(half // 2, half // 2)}

    def head_copy(p, at, sems, k, device):
        block = wh.at[p, :, at]
        copy = pltpu.make_async_remote_copy(
            src_ref=block,
            dst_ref=block,
            send_sem=sems.at[0, k],
            recv_sem=sems.at[1, k],
            device_id=device,
            device_id_type=MESH,
        )
        copy.start()
        return copy

    def spread():
        return [
            head_copy(x, whole, bsem.at[0], k, (me, lax.rem(x + k, parts))) for k in (1, 3)
        ]

    def relay(arrivals):
        sent, handed = [], []
        for copy, k in zip(arrivals, (1, 3)):
            copy.wait_recv()
            p = lax.rem(x + parts - k, parts)
            sent.append(head_copy(p, quarters[k], bsem.at[1], k, (me, lax.rem(x + k, parts))))
            handed.append(head_copy(p, whole, fsem.at[0], k, (sibling, x)))
        return sent, handed

    def spread_small():
        copies = []
        for i, (src, dst) in enumerate(
            (
                (head_bias_in, head_bias_all),
                (value_weight_in, value_weight_all),
                (adv_weight_in, adv_weight_all),
            )
        ):
            for k in range(1, parts):
                copy = pltpu.make_async_remote_copy(
                    src_ref=src,
                    dst_ref=dst.at[x],
                    send_sem=ssem.at[i, 0, k],
                    recv_sem=ssem.at[i, 1, k],
                    device_id=(me, lax.rem(x + k, parts)),
                    device_id_type=MESH,
                )
                copy.start()
                copies.append(copy)
        return copies

    def over_parts(ref, copies, add):
        add(x, ref[x])
        for copy, k in zip(copies[1:] + copies[:1], (3, 1, 2)):
            copy.wait_recv()
            p = lax.rem(x + k, parts)
            add(p, ref[p])

    to_group(obs_send, obs_recv, 0)
    loads[4].wait()
    hid_copies = to_parts(hid_all, 0)
    small_copies = spread_small()
    near = spread()
    loads[5].wait()
    regroup(wi_raw, wi)
    loads[3].wait()
    regroup(ws_raw, ws)
    for load in loads[7:]:
        load.wait()
    gate = [jnp.broadcast_to(gate_bias_ref[g : g + 1, :], (own, units)) for g in range(4)]

    def add_state(p, block):
        at = pl.ds(pl.multiple_of(p * units, units), units)
        for g in range(4):
            gate[g] = gate[g] + dot(block, ws[g, at, :])

    over_parts(hid_all, hid_copies, add_state)
    bias = adv_bias_ref[...]
    bias = value_bias_ref[0] + bias - jnp.mean(bias, axis=1, keepdims=True)

    val_send[...] = jnp.zeros((groups, 128), F32)

    drain(obs_recv, 1)
    obs_all[x] = dot(batch_hot, obs_recv[...].astype(BF16)).astype(BF16)
    obs_copies = to_parts(obs_all, 1)
    far, handed = relay(near)

    def add_input(p, block):
        at = pl.ds(pl.multiple_of(p * features, features), features)
        for g in range(4):
            gate[g] = gate[g] + dot(block, wi[g, at, :])

    over_parts(obs_all, obs_copies, add_input)
    cell = jax.nn.sigmoid(gate[1]) * cell_ref[...].astype(F32) + jax.nn.sigmoid(
        gate[0]
    ) * jnp.tanh(gate[2])
    hidden = (jax.nn.sigmoid(gate[3]) * jnp.tanh(cell)).astype(BF16)
    new_all[x] = hidden
    new_copies = to_parts(new_all, 2)
    hidden_out[...] = hidden
    cell_out[...] = cell.astype(BF16)
    for copy in far:
        copy.wait_recv()
    handed.append(head_copy(lax.rem(x + 2, parts), whole, fsem.at[0], 2, (sibling, x)))
    for copy in small_copies:
        copy.wait_recv()
    for copy in handed:
        copy.wait_recv()
    stream = [
        [jnp.broadcast_to(head_bias_all[p, i : i + 1, :], (own, head_units)) for p in range(parts)]
        for i in range(2)
    ]

    def add_head(p, block):
        at = pl.ds(pl.multiple_of(p * units, units), units)
        for i in range(2):
            for j in range(parts):
                stream[i][j] = stream[i][j] + dot(block, wh[j, i, at, :])

    over_parts(new_all, new_copies, add_head)
    stream = [[jnp.maximum(s, 0.0).astype(BF16) for s in part] for part in stream]
    value = jnp.zeros((own, head_units), F32)
    advantage = jnp.zeros((own, actions), F32)
    for p in range(parts):
        value = value + stream[0][p].astype(F32) * value_weight_all[p].astype(F32)
        advantage = advantage + dot(stream[1][p], adv_weight_all[p], NT)
    value = jnp.sum(value, axis=1, keepdims=True)
    values = value + advantage - jnp.mean(advantage, axis=1, keepdims=True) + bias
    val_send[:, 0:actions] = pick(batch_t[...], values)
    to_group(val_send, val_recv, 2)
    for copies in (hid_copies, obs_copies, new_copies, small_copies, near, far, handed):
        for copy in copies:
            copy.wait_send()
    drain(obs_send, 0)
    drain(val_send, 2)
    drain(val_recv, 3)
    q_out[...] = pick(slot_t[...], val_recv[...])


def out_kernel(q_ref, hidden_ref, cell_ref, q_out, hidden_out, cell_out):
    hidden_out[...] = hidden_ref[...]
    cell_out[...] = cell_ref[...]
    q_out[...] = q_ref[...].T[0 : q_out.shape[0]]


def farthest_first(groups):
    side = 8
    ring = lambda d: min(d, side - d)
    moves = [(dz, dy, dc) for dz in range(side) for dy in range(side) for dc in range(2)]
    moves.sort(key=lambda m: -10 * (ring(m[0]) + ring(m[1])) - m[2])

    def peer(dz, dy, dc):
        def index(me):
            z, y, c = me // (2 * side), lax.rem(me // 2, side), lax.rem(me, 2)
            z, y, c = lax.rem(z + dz, side), lax.rem(y + dy, side), lax.rem(c + dc, 2)
            return (z * side + y) * 2 + c

        return index

    assert len(moves) == groups
    return [peer(*m) for m in moves if any(m)]


def solution(mesh):
    groups, parts = mesh.shape["group"], mesh.shape["mp"]

    def per_device(
        observations,
        hidden_state,
        cell_state,
        arrival_order,
        batch_counts,
        input_weight,
        state_weight,
        gate_bias,
        head_weight,
        head_bias,
        value_weight,
        value_bias,
        advantage_weight,
        advantage_bias,
    ):
        slots, features = observations.shape
        own, units = hidden_state.shape
        head_units = head_bias.shape[1]
        actions = advantage_weight.shape[1]
        vmem = pl.BlockSpec(memory_space=pltpu.VMEM)
        smem = pl.BlockSpec(memory_space=pltpu.SMEM)
        hbm = pl.BlockSpec(memory_space=pltpu.HBM)
        dma = pltpu.SemaphoreType.DMA

        def as_stored(w):
            return w.reshape(-1, 4, 2, 128).transpose(0, 2, 1, 3).reshape(-1, 8, 128)

        wi, ws = as_stored(input_weight), as_stored(state_weight)
        order = arrival_order.reshape(-1, 128)
        counts = batch_counts.reshape(1, -1)
        vw, aw, ab = value_weight.T, advantage_weight.T, advantage_bias.reshape(1, -1)
        like = lambda a: pltpu.VMEM(a.shape, a.dtype)
        q, new_hidden, new_cell = pl.pallas_call(
            functools.partial(step_kernel, groups, parts, farthest_first(groups)),
            name="acting_step",
            out_shape=(
                jax.ShapeDtypeStruct((slots, 128), F32),
                jax.ShapeDtypeStruct((own, units), BF16),
                jax.ShapeDtypeStruct((own, units), BF16),
            ),
            in_specs=[hbm] * 11 + [smem] + [hbm] * 2,
            out_specs=(vmem,) * 3,
            scratch_shapes=[
                like(observations),
                like(cell_state),
                like(order),
                like(counts),
                like(gate_bias),
                *(pltpu.VMEM((parts, *a.shape), a.dtype) for a in (head_bias, vw, aw)),
                like(ab),
                like(wi),
                like(ws),
                like(head_weight),
                pltpu.VMEM((4, wi.shape[0], units), BF16),
                pltpu.VMEM((4, ws.shape[0], units), BF16),
                pltpu.VMEM((parts, 2, head_weight.shape[0], head_units), BF16),
                pltpu.VMEM((groups, features), F32),
                pltpu.VMEM((groups, features), F32),
                pltpu.VMEM((parts, own, features), BF16),
                pltpu.VMEM((parts, own, units), BF16),
                pltpu.VMEM((parts, own, units), BF16),
                pltpu.VMEM((groups, 128), F32),
                pltpu.VMEM((groups, 128), F32),
                pltpu.VMEM((groups, own), BF16),
                pltpu.VMEM((slots, groups), BF16),
                dma((13,)),
                dma((4,)),
                dma((3, 2, parts)),
                dma((3, 2, parts)),
                dma((2, 2, parts)),
                dma((2, 2, parts)),
            ],
            compiler_params=pltpu.CompilerParams(
                collective_id=0, has_side_effects=True, vmem_limit_bytes=32 * 2**20
            ),
        )(
            *(
                a if a is value_bias else pltpu.with_memory_space_constraint(a, pltpu.HBM)
                for a in (
                    observations,
                    hidden_state,
                    cell_state,
                    order,
                    counts,
                    wi,
                    ws,
                    gate_bias,
                    head_weight,
                    head_bias,
                    vw,
                    value_bias,
                    aw,
                    ab,
                )
            )
        )
        q, new_hidden, new_cell = pl.pallas_call(
            out_kernel,
            name="outputs",
            out_shape=(
                jax.ShapeDtypeStruct((actions, slots), F32),
                jax.ShapeDtypeStruct((own, units), BF16),
                jax.ShapeDtypeStruct((own, units), BF16),
            ),
            in_specs=[vmem] * 3,
            out_specs=(vmem,) * 3,
            compiler_params=pltpu.CompilerParams(vmem_limit_bytes=4 * 2**20),
        )(q, new_hidden, new_cell)
        return q.T, new_hidden, new_cell

    placed = (
        P("group", "mp"),
        P("group", "mp"),
        P("group", "mp"),
        P(),
        P(),
        P(None, None, "mp"),
        P(None, None, "mp"),
        P(None, "mp"),
        P(None, None, "mp"),
        P(None, "mp"),
        P("mp", None),
        P(),
        P("mp", None),
        P(),
    )
    return jax.shard_map(
        per_device,
        mesh=mesh,
        in_specs=placed,
        out_specs=(P("group", None), P("group", "mp"), P("group", "mp")),
        check_vma=False,
    )
```

```python
import functools

import jax
import jax.numpy as jnp
from jax import lax
from jax.experimental import pallas as pl
from jax.experimental.pallas import tpu as pltpu
from jax.sharding import PartitionSpec as P

MESH = pl.DeviceIdType.MESH
F32 = jnp.float32
BF16 = jnp.bfloat16
NT = (((1,), (1,)), ((), ()))


def iota(shape, dim):
    return lax.broadcasted_iota(jnp.int32, shape, dim)


NN = (((1,), (0,)), ((), ()))


def dot(a, b, dims=NN):
    return lax.dot_general(a, b, dims, preferred_element_type=F32)


def pick(table, values):
    high = values.astype(BF16)
    rest = values - high.astype(F32)
    mid = rest.astype(BF16)
    low = (rest - mid.astype(F32)).astype(BF16)
    return dot(table, high) + dot(table, mid) + dot(table, low)


def regroup(src, dst):
    gates = dst.shape[0]
    block = 16

    def body(i, carry):
        at = pl.multiple_of(i * block, block)
        v = src[pl.ds(at, block)].astype(F32)
        t = pltpu.einshape("kjn->jkn", v).astype(BF16)
        for j in range(v.shape[1]):
            half, g = divmod(j, gates)
            dst[g, pl.ds(at, block), half * 128 : half * 128 + 128] = t[j]
        return carry

    lax.fori_loop(0, src.shape[0] // block, body, 0, unroll=4)


def step_kernel(
    groups,
    parts,
    peers,
    obs_in,
    hidden_in,
    cell_in,
    order_in,
    counts_in,
    wi_in,
    ws_in,
    gate_bias_in,
    wh_in,
    head_bias_in,
    value_weight_in,
    value_bias_ref,
    adv_weight_in,
    adv_bias_in,
    q_out,
    hidden_out,
    cell_out,
    obs_ref,
    cell_ref,
    order_ref,
    counts_ref,
    gate_bias_ref,
    head_bias_all,
    value_weight_all,
    adv_weight_all,
    adv_bias_ref,
    wi_raw,
    ws_raw,
    wh_raw,
    wi,
    ws,
    wh,
    obs_send,
    obs_recv,
    obs_all,
    hid_all,
    new_all,
    val_send,
    val_recv,
    batch_t,
    slot_t,
    lsem,
    gsem,
    xsem,
    ssem,
    bsem,
    fsem,
):
    me = lax.axis_index("group")
    x = lax.axis_index("mp")
    own = hidden_in.shape[0]
    slots = obs_ref.shape[0]
    features = obs_ref.shape[1]
    units = cell_ref.shape[1]
    head_units = head_bias_all.shape[2]
    actions = adv_weight_all.shape[1]
    core = lax.rem(me, 2)
    sibling = me + 1 - 2 * core
    half = wh_in.shape[0] // 2

    loads = [
        pltpu.make_async_copy(src, dst, lsem.at[i])
        for i, (src, dst) in enumerate(
            (
                (order_in, order_ref),
                (counts_in, counts_ref),
                (obs_in, obs_ref),
                (ws_in, ws_raw),
                (hidden_in, hid_all.at[x]),
                (wi_in, wi_raw),
                (wh_in, wh_raw),
                (cell_in, cell_ref),
                (gate_bias_in, gate_bias_ref),
                (head_bias_in, head_bias_all.at[x]),
                (value_weight_in, value_weight_all.at[x]),
                (adv_weight_in, adv_weight_all.at[x]),
                (adv_bias_in, adv_bias_ref),
            )
        )
    ]
    for load in loads[:3]:
        load.start()
    barrier = pltpu.get_barrier_semaphore()
    others = [peer(me) for peer in peers]
    for other in others:
        pl.semaphore_signal(barrier, inc=1, device_id=(other, x), device_id_type=MESH)
    for k in range(1, parts):
        pl.semaphore_signal(
            barrier, inc=1, device_id=(me, lax.rem(x + k, parts)), device_id_type=MESH
        )
    for load in loads[3:]:
        load.start()

    loads[0].wait()
    loads[1].wait()
    counts = jnp.broadcast_to(counts_ref[...], (8, groups))
    before = (iota((groups, groups), 0) < iota((groups, groups), 1)).astype(BF16)
    starts = dot(counts.astype(BF16), before).astype(jnp.int32)[0:1]
    ends = starts + counts[0:1]
    mine = iota((1, groups), 1) == me
    start = jnp.sum(jnp.where(mine, starts, 0), axis=1, keepdims=True)
    count = jnp.sum(jnp.where(mine, counts[0:1], 0), axis=1, keepdims=True)
    order = order_ref[...]
    rows = order.shape[0]
    first = start // 128
    row_of = iota((rows, 128), 0)
    owners, places = [], []
    for j in range(2):
        window = jnp.sum(jnp.where(row_of == first + j, order, 0), axis=0, keepdims=True)
        place = (first + j) * 128 + iota((1, 128), 1) - start
        real = (place >= 0) & (place < count)
        owners.append(jnp.where(real, window // own, -1))
        places.append(place)
    owner_hot = jnp.concatenate([iota((groups, 128), 0) == o for o in owners], axis=1)
    place_hot = jnp.concatenate([iota((slots, 128), 0) == p for p in places], axis=1)
    owner_hot = owner_hot.astype(BF16)
    place_hot = place_hot.astype(BF16)
    slot_of = dot(owner_hot, place_hot, NT).astype(BF16)
    slot_t[...] = dot(place_hot, owner_hot, NT).astype(BF16)
    loads[2].wait()
    obs_send[...] = dot(slot_of, obs_ref[...])

    local = order - me * own
    lane = iota((own, 128), 1)
    sub = iota((own, 128), 0)
    total = jnp.zeros((own, 128), jnp.int32)
    for r in range(rows):
        total = total + jnp.where(local[r : r + 1] == sub, lane + r * 128, 0)
    position = jnp.sum(total, axis=1, keepdims=True)
    batch_hot = ((position >= starts) & (position < ends)).astype(F32)
    batch_t[...] = batch_hot.T.astype(BF16)
    batch_hot = batch_hot.astype(BF16)

    loads[6].wait()
    for i in range(2):
        wh[x, i] = wh_raw[:, i, :]
    pl.semaphore_wait(barrier, groups + parts - 2)

    def to_group(src, dst, s):
        for other in others:
            pltpu.make_async_remote_copy(
                src_ref=src.at[pl.ds(other, 1)],
                dst_ref=dst.at[pl.ds(me, 1)],
                send_sem=gsem.at[s],
                recv_sem=gsem.at[s + 1],
                device_id=(other, x),
                device_id_type=MESH,
            ).start()
        dst[pl.ds(me, 1), :] = src[pl.ds(me, 1), :]

    def drain(ref, s):
        some = ref.at[pl.ds(0, groups - 1)]
        pltpu.make_async_copy(some, some, gsem.at[s]).wait()

    def to_parts(ref, s):
        copies = []
        for k in (2, 1, 3):
            copy = pltpu.make_async_remote_copy(
                src_ref=ref.at[x],
                dst_ref=ref.at[x],
                send_sem=xsem.at[s, 0, k],
                recv_sem=xsem.at[s, 1, k],
                device_id=(me, lax.rem(x + k, parts)),
                device_id_type=MESH,
            )
            copy.start()
            copies.append(copy)
        return copies

    def rows_at(first, count):
        return pl.ds(pl.multiple_of(core * half + first, count), count)

    whole = rows_at(0, half)
    quarters = {1: rows_at(0, half // 2), 3: rows_at(half // 2, half // 2)}

    def head_copy(p, at, sems, k, device):
        block = wh.at[p, :, at]
        copy = pltpu.make_async_remote_copy(
            src_ref=block,
            dst_ref=block,
            send_sem=sems.at[0, k],
            recv_sem=sems.at[1, k],
            device_id=device,
            device_id_type=MESH,
        )
        copy.start()
        return copy

    def spread():
        return [
            head_copy(x, whole, bsem.at[0], k, (me, lax.rem(x + k, parts))) for k in (1, 3)
        ]

    def relay(arrivals):
        sent, handed = [], []
        for copy, k in zip(arrivals, (1, 3)):
            copy.wait_recv()
            p = lax.rem(x + parts - k, parts)
            sent.append(head_copy(p, quarters[k], bsem.at[1], k, (me, lax.rem(x + k, parts))))
            handed.append(head_copy(p, whole, fsem.at[0], k, (sibling, x)))
        return sent, handed

    def spread_small():
        copies = []
        for i, (src, dst) in enumerate(
            (
                (head_bias_in, head_bias_all),
                (value_weight_in, value_weight_all),
                (adv_weight_in, adv_weight_all),
            )
        ):
            for k in range(1, parts):
                copy = pltpu.make_async_remote_copy(
                    src_ref=src,
                    dst_ref=dst.at[x],
                    send_sem=ssem.at[i, 0, k],
                    recv_sem=ssem.at[i, 1, k],
                    device_id=(me, lax.rem(x + k, parts)),
                    device_id_type=MESH,
                )
                copy.start()
                copies.append(copy)
        return copies

    def over_parts(ref, copies, add):
        add(x, ref[x])
        for copy, k in zip(copies[1:] + copies[:1], (3, 1, 2)):
            copy.wait_recv()
            p = lax.rem(x + k, parts)
            add(p, ref[p])

    near = spread()
    to_group(obs_send, obs_recv, 0)
    loads[4].wait()
    hid_copies = to_parts(hid_all, 0)
    small_copies = spread_small()
    loads[5].wait()
    regroup(wi_raw, wi)
    loads[3].wait()
    regroup(ws_raw, ws)
    for load in loads[7:]:
        load.wait()
    gate = [jnp.broadcast_to(gate_bias_ref[g : g + 1, :], (own, units)) for g in range(4)]

    def add_state(p, block):
        at = pl.ds(pl.multiple_of(p * units, units), units)
        for g in range(4):
            gate[g] = gate[g] + dot(block, ws[g, at, :])

    bias = adv_bias_ref[...]
    bias = value_bias_ref[0] + bias - jnp.mean(bias, axis=1, keepdims=True)

    val_send[...] = jnp.zeros((groups, 128), F32)

    drain(obs_recv, 1)
    obs_all[x] = dot(batch_hot, obs_recv[...].astype(BF16)).astype(BF16)
    obs_copies = to_parts(obs_all, 1)
    far, handed = relay(near)
    over_parts(hid_all, hid_copies, add_state)

    def add_input(p, block):
        at = pl.ds(pl.multiple_of(p * features, features), features)
        for g in range(4):
            gate[g] = gate[g] + dot(block, wi[g, at, :])

    over_parts(obs_all, obs_copies, add_input)
    cell = jax.nn.sigmoid(gate[1]) * cell_ref[...].astype(F32) + jax.nn.sigmoid(
        gate[0]
    ) * jnp.tanh(gate[2])
    hidden = (jax.nn.sigmoid(gate[3]) * jnp.tanh(cell)).astype(BF16)
    new_all[x] = hidden
    new_copies = to_parts(new_all, 2)
    hidden_out[...] = hidden
    cell_out[...] = cell.astype(BF16)
    for copy in far:
        copy.wait_recv()
    handed.append(head_copy(lax.rem(x + 2, parts), whole, fsem.at[0], 2, (sibling, x)))
    for copy in small_copies:
        copy.wait_recv()
    for copy in handed:
        copy.wait_recv()
    stream = [
        [jnp.broadcast_to(head_bias_all[p, i : i + 1, :], (own, head_units)) for p in range(parts)]
        for i in range(2)
    ]

    def add_head(p, block):
        at = pl.ds(pl.multiple_of(p * units, units), units)
        for i in range(2):
            for j in range(parts):
                stream[i][j] = stream[i][j] + dot(block, wh[j, i, at, :])

    over_parts(new_all, new_copies, add_head)
    stream = [[jnp.maximum(s, 0.0).astype(BF16) for s in part] for part in stream]
    value = jnp.zeros((own, head_units), F32)
    advantage = jnp.zeros((own, actions), F32)
    for p in range(parts):
        value = value + stream[0][p].astype(F32) * value_weight_all[p].astype(F32)
        advantage = advantage + dot(stream[1][p], adv_weight_all[p], NT)
    value = jnp.sum(value, axis=1, keepdims=True)
    values = value + advantage - jnp.mean(advantage, axis=1, keepdims=True) + bias
    val_send[:, 0:actions] = pick(batch_t[...], values)
    to_group(val_send, val_recv, 2)
    for copies in (hid_copies, obs_copies, new_copies, small_copies, near, far, handed):
        for copy in copies:
            copy.wait_send()
    drain(obs_send, 0)
    drain(val_send, 2)
    drain(val_recv, 3)
    q_out[...] = pick(slot_t[...], val_recv[...])


def out_kernel(q_ref, hidden_ref, cell_ref, q_out, hidden_out, cell_out):
    hidden_out[...] = hidden_ref[...]
    cell_out[...] = cell_ref[...]
    q_out[...] = q_ref[...].T[0 : q_out.shape[0]]


def farthest_first(groups):
    side = 8
    ring = lambda d: min(d, side - d)
    moves = [(dz, dy, dc) for dz in range(side) for dy in range(side) for dc in range(2)]
    moves.sort(key=lambda m: -10 * (ring(m[0]) + ring(m[1])) - m[2])

    def peer(dz, dy, dc):
        def index(me):
            z, y, c = me // (2 * side), lax.rem(me // 2, side), lax.rem(me, 2)
            z, y, c = lax.rem(z + dz, side), lax.rem(y + dy, side), lax.rem(c + dc, 2)
            return (z * side + y) * 2 + c

        return index

    assert len(moves) == groups
    return [peer(*m) for m in moves if any(m)]


def solution(mesh):
    groups, parts = mesh.shape["group"], mesh.shape["mp"]

    def per_device(
        observations,
        hidden_state,
        cell_state,
        arrival_order,
        batch_counts,
        input_weight,
        state_weight,
        gate_bias,
        head_weight,
        head_bias,
        value_weight,
        value_bias,
        advantage_weight,
        advantage_bias,
    ):
        slots, features = observations.shape
        own, units = hidden_state.shape
        head_units = head_bias.shape[1]
        actions = advantage_weight.shape[1]
        vmem = pl.BlockSpec(memory_space=pltpu.VMEM)
        smem = pl.BlockSpec(memory_space=pltpu.SMEM)
        hbm = pl.BlockSpec(memory_space=pltpu.HBM)
        dma = pltpu.SemaphoreType.DMA

        def as_stored(w):
            return w.reshape(-1, 4, 2, 128).transpose(0, 2, 1, 3).reshape(-1, 8, 128)

        wi, ws = as_stored(input_weight), as_stored(state_weight)
        order = arrival_order.reshape(-1, 128)
        counts = batch_counts.reshape(1, -1)
        vw, aw, ab = value_weight.T, advantage_weight.T, advantage_bias.reshape(1, -1)
        like = lambda a: pltpu.VMEM(a.shape, a.dtype)
        q, new_hidden, new_cell = pl.pallas_call(
            functools.partial(step_kernel, groups, parts, farthest_first(groups)),
            name="acting_step",
            out_shape=(
                jax.ShapeDtypeStruct((slots, 128), F32),
                jax.ShapeDtypeStruct((own, units), BF16),
                jax.ShapeDtypeStruct((own, units), BF16),
            ),
            in_specs=[hbm] * 11 + [smem] + [hbm] * 2,
            out_specs=(vmem,) * 3,
            scratch_shapes=[
                like(observations),
                like(cell_state),
                like(order),
                like(counts),
                like(gate_bias),
                *(pltpu.VMEM((parts, *a.shape), a.dtype) for a in (head_bias, vw, aw)),
                like(ab),
                like(wi),
                like(ws),
                like(head_weight),
                pltpu.VMEM((4, wi.shape[0], units), BF16),
                pltpu.VMEM((4, ws.shape[0], units), BF16),
                pltpu.VMEM((parts, 2, head_weight.shape[0], head_units), BF16),
                pltpu.VMEM((groups, features), F32),
                pltpu.VMEM((groups, features), F32),
                pltpu.VMEM((parts, own, features), BF16),
                pltpu.VMEM((parts, own, units), BF16),
                pltpu.VMEM((parts, own, units), BF16),
                pltpu.VMEM((groups, 128), F32),
                pltpu.VMEM((groups, 128), F32),
                pltpu.VMEM((groups, own), BF16),
                pltpu.VMEM((slots, groups), BF16),
                dma((13,)),
                dma((4,)),
                dma((3, 2, parts)),
                dma((3, 2, parts)),
                dma((2, 2, parts)),
                dma((2, 2, parts)),
            ],
            compiler_params=pltpu.CompilerParams(
                collective_id=0, has_side_effects=True, vmem_limit_bytes=32 * 2**20
            ),
        )(
            *(
                a if a is value_bias else pltpu.with_memory_space_constraint(a, pltpu.HBM)
                for a in (
                    observations,
                    hidden_state,
                    cell_state,
                    order,
                    counts,
                    wi,
                    ws,
                    gate_bias,
                    head_weight,
                    head_bias,
                    vw,
                    value_bias,
                    aw,
                    ab,
                )
            )
        )
        q, new_hidden, new_cell = pl.pallas_call(
            out_kernel,
            name="outputs",
            out_shape=(
                jax.ShapeDtypeStruct((actions, slots), F32),
                jax.ShapeDtypeStruct((own, units), BF16),
                jax.ShapeDtypeStruct((own, units), BF16),
            ),
            in_specs=[vmem] * 3,
            out_specs=(vmem,) * 3,
            compiler_params=pltpu.CompilerParams(vmem_limit_bytes=4 * 2**20),
        )(q, new_hidden, new_cell)
        return q.T, new_hidden, new_cell

    placed = (
        P("group", "mp"),
        P("group", "mp"),
        P("group", "mp"),
        P(),
        P(),
        P(None, None, "mp"),
        P(None, None, "mp"),
        P(None, "mp"),
        P(None, None, "mp"),
        P(None, "mp"),
        P("mp", None),
        P(),
        P("mp", None),
        P(),
    )
    return jax.shard_map(
        per_device,
        mesh=mesh,
        in_specs=placed,
        out_specs=(P("group", None), P("group", "mp"), P("group", "mp")),
        check_vma=False,
    )
```
